32 devices in a mesh: groups: 2 (over y), row: 8 (over z, x), col: 2 (over core).
Axes of the slice: x: 2, y: 2, z: 4, core: 2. Of those that a mesh axis runs over, the one named last changes fastest.
Arguments:
- wavenumber: float32 [2], P('groups'), parts along dimension 0, may hold values from 30 to 90
- tgt_geom: float32 [6, 4096], P(None, ('groups', 'row')), parts along dimension 1, may hold values from -2 to 8, as said below
- src_geom: float32 [4, 512], P(None, ('groups', 'row', 'col')), parts along dimension 1, may hold values from -2 to 8, as said below
- excite: bfloat16 [128, 512], P(None, ('groups', 'row', 'col')), parts along dimension 1, may hold values from -6 to 6
- tgt_nodes: float32 [3, 6144], P(None, ('groups', 'row')), parts along dimension 1, may hold values from -2 to 8, as said below
- src_nodes: float32 [3, 3072], P(None, ('groups', 'row')), parts along dimension 1, may hold values from -2 to 8, as said below
- tgt_weights: bfloat16 [2, 192, 4096], P(None, None, ('groups', 'row')), parts along dimension 2, may hold values from -0.109375 to 0.109375
- src_weights: bfloat16 [2, 192, 512], P(None, None, ('groups', 'row', 'col')), parts along dimension 2, may hold values from -1 to 1
- near_order: int32 [32, 9], P(('groups', 'row')), parts along dimension 0, may hold values from 0 to 3
Outputs:
- responses: float32 [4096, 128], P(('groups', 'row', 'col')), parts along dimension 0
The draws below stay inside these ranges and needn't reach their ends.
There are 2 independent parts, one for each index of `groups`. The reference program is written for one: setup_inputs(seed, part) draws one part's arguments, and reference() takes and returns one part's arrays. A program takes and returns all parts, laid end to end along the dimension named above; each array names one. Nothing has to cross between parts.
Inputs may be any that keep to these rules, and one draw needn't show every extreme that they name: `tgt_geom`: rows 0 to 2 are points, rows 3 to 5 unit normals. `src_geom`: rows 0 to 2 are points, row 3 positive areas. `tgt_nodes`: Points. `src_nodes`: Points. `near_order`: 0 marks a pair that is not near.
All inputs are finite; a program needn't handle non-finite values.
Results may differ from the reference program's by a relative error of at most 0.0011.
Values may be sent and summed in bfloat16 or wider, within the bound.
A program may use at most 64 MiB of HBM per device.

```python
import jax
import jax.numpy as jnp
from jax import lax

BLK = 128
RBD = 2
CPD = 16
NEXC = 64
QSTEP = 64
ORDERS = 3
NEARW = 4
QN = 192
NBAND = 9
NROWS = 2048
NCOL = 256
N_ROW = 8


ACROSS = 2.0


def line_positions(key, count, per_unit):
    first, second = jax.random.split(key)
    along = (jnp.arange(count, dtype=jnp.float32) + jax.random.uniform(first, (count,), jnp.float32)) / per_unit
    across = jax.random.uniform(second, (2, count), jnp.float32, -ACROSS, ACROSS)
    return jnp.concatenate([along[None, :], across], 0)


def draw_tgt_geom(key, part):
    place_key, normal_key = jax.random.split(jax.random.fold_in(key, 11))
    points = line_positions(place_key, NROWS, BLK * RBD)
    raw = jax.random.normal(normal_key, (3, NROWS), jnp.float32)
    length = jnp.sqrt(jnp.sum(raw * raw, 0, keepdims=True))
    return jnp.concatenate([points, raw / jnp.maximum(length, 0.001)], 0)


def draw_src_geom(key, part):
    place_key, area_key = jax.random.split(jax.random.fold_in(key, 23))
    points = line_positions(place_key, NCOL, NCOL * BLK * RBD // NROWS)
    areas = jnp.exp(jax.random.uniform(area_key, (1, NCOL), jnp.float32, jnp.log(0.1), jnp.log(0.4)))
    return jnp.concatenate([points, areas], 0)


def draw_tgt_nodes(key, part):
    return line_positions(jax.random.fold_in(key, 37), QN * NROWS // BLK, QN * RBD)


def draw_src_nodes(key, part):
    return line_positions(jax.random.fold_in(key, 41), QN * NROWS // (BLK * RBD), QN)


def plant(values, key, smallest, largest):
    extent = values.shape
    index_at = [jax.random.randint(jax.random.fold_in(key, axis), (), 0, extent[axis]) for axis in range(len(extent))]
    values = values.at[tuple(index_at)].set(smallest)
    longest = extent.index(max(extent))
    index_at[longest] = (index_at[longest] + 1) % extent[longest]
    return values.at[tuple(index_at)].set(largest)


def levels(rng, shape, shards, low, largest):
    loudness, own = 1.0, jax.random.fold_in(rng, 6)
    for position, shards_of in shards:
        steps = jnp.exp(jax.random.uniform(jax.random.fold_in(own, position), (shards_of,), jnp.float32, low / len(shards), largest / len(shards)))
        loudness = loudness * jnp.repeat(steps, shape[position] // shards_of).reshape([-1 if axis == position else 1 for axis in range(len(shape))])
    return loudness


def noise(rng, extent, deviation, most, pieces=(), kind=jnp.bfloat16):
    array = deviation * jax.random.normal(rng, extent, jnp.float32)
    if pieces:
        array = array * levels(rng, extent, pieces, -0.22, 0.18)
    return jnp.clip(array, -most, most).astype(kind)


def setup_inputs(seed: int = 0, part: int = 0) -> dict:
    seeds = jax.random.split(jax.random.key(seed), 10)
    part_splits = jax.random.split(jax.random.fold_in(seeds[9], part), 10)
    return {
        "wavenumber": jnp.clip(jax.random.uniform(part_splits[0], (1,), jnp.float32, 30.0, 90.0), 30.0, 90.0),
        "tgt_geom": draw_tgt_geom(jax.random.fold_in(jax.random.fold_in(seeds[9], part), 71), part),
        "src_geom": draw_src_geom(jax.random.fold_in(jax.random.fold_in(seeds[9], part), 71), part),
        "excite": noise(part_splits[3], (2 * NEXC, NCOL), 1.0, 6.0, ((1, 16),)),
        "tgt_nodes": draw_tgt_nodes(jax.random.fold_in(jax.random.fold_in(seeds[9], part), 71), part),
        "src_nodes": draw_src_nodes(jax.random.fold_in(jax.random.fold_in(seeds[9], part), 71), part),
        "tgt_weights": noise(part_splits[6], (2, QN, NROWS), (16 * QN) ** -0.5, 0.109375, ((2, 8),)),
        "src_weights": noise(part_splits[7], (2, QN, NCOL), (2 * CPD) ** -0.5, 1.0, ((2, 16),)),
        "near_order": plant(jax.random.randint(part_splits[8], (N_ROW * RBD, NBAND), 0, ORDERS + 1), jax.random.fold_in(part_splits[8], 1), 0, ORDERS).astype(jnp.int32),
    }


SOFT = 0.05
FOUR_PI = 4.0 * 3.141592653589793
HIGH = lax.Precision.HIGHEST

def far_block(targets, sources, excite_cols, wave_number):
    delta_x = targets[0][:, None] - sources[0][None, :]
    delta_y = targets[1][:, None] - sources[1][None, :]
    delta_z = targets[2][:, None] - sources[2][None, :]
    radius = jnp.sqrt(delta_x * delta_x + delta_y * delta_y + delta_z * delta_z + SOFT * SOFT)
    cosine = (targets[3][:, None] * delta_x + targets[4][:, None] * delta_y + targets[5][:, None] * delta_z) / radius
    scale = sources[3][None, :] / (FOUR_PI * radius)
    phase = wave_number * radius
    green_re = scale * jnp.cos(phase)
    green_im = scale * jnp.sin(phase)
    factor_re = 1.0 - cosine
    factor_im = -cosine / phase
    kern_re = (green_re * factor_re - green_im * factor_im).astype(jnp.bfloat16)
    kern_im = (green_re * factor_im + green_im * factor_re).astype(jnp.bfloat16)
    dims = (((1,), (1,)), ((), ()))
    first = lax.dot_general(kern_re, excite_cols, dims, preferred_element_type=jnp.float32)
    second = lax.dot_general(kern_im, excite_cols, dims, preferred_element_type=jnp.float32)
    half = excite_cols.shape[0] // 2
    return jnp.concatenate([first[:, :half] - second[:, half:], first[:, half:] + second[:, :half]], 1)

def near_term(tnodes, snodes, moments, unodes, order_val, wave_number):
    delta_x = tnodes[0][:, None] - snodes[0][None, :]
    delta_y = tnodes[1][:, None] - snodes[1][None, :]
    delta_z = tnodes[2][:, None] - snodes[2][None, :]
    radius = jnp.sqrt(delta_x * delta_x + delta_y * delta_y + delta_z * delta_z + SOFT * SOFT)
    scale = 1.0 / (FOUR_PI * radius)
    node_live = (jnp.arange(QN, dtype=jnp.int32) < order_val * QSTEP).astype(jnp.float32)
    node_mask = node_live[:, None] * node_live[None, :]
    green_re = scale * jnp.cos(wave_number * radius) * node_mask
    green_im = scale * jnp.sin(wave_number * radius) * node_mask
    half = moments.shape[1] // 2
    mom_re = moments[:, :half]
    mom_im = moments[:, half:]
    inner_re = jnp.dot(green_re, mom_re, precision=HIGH) - jnp.dot(green_im, mom_im, precision=HIGH)
    inner_im = jnp.dot(green_re, mom_im, precision=HIGH) + jnp.dot(green_im, mom_re, precision=HIGH)
    test_re = unodes[0].astype(jnp.float32)
    test_im = unodes[1].astype(jnp.float32)
    dims = (((0,), (0,)), ((), ()))
    out_re = lax.dot_general(test_re, inner_re, dims, precision=HIGH) - lax.dot_general(test_im, inner_im, dims, precision=HIGH)
    out_im = lax.dot_general(test_re, inner_im, dims, precision=HIGH) + lax.dot_general(test_im, inner_re, dims, precision=HIGH)
    return jnp.concatenate([out_re, out_im], 1)

def reference(wavenumber, tgt_geom, src_geom, excite, tgt_nodes, src_nodes, tgt_weights, src_weights, near_order):
    wave_number = wavenumber[0]
    row_blocks = NROWS // BLK
    col_blocks = row_blocks // RBD
    cols_block = NCOL // col_blocks
    half = excite.shape[0] // 2

    def moment(index):
        start = (index * cols_block).astype(jnp.int32)
        weights = lax.dynamic_slice_in_dim(src_weights, start, cols_block, 2)
        cols = lax.dynamic_slice_in_dim(excite, start, cols_block, 1)
        dims = (((1,), (1,)), ((), ()))
        first = lax.dot_general(weights[0], cols, dims, preferred_element_type=jnp.float32)
        second = lax.dot_general(weights[1], cols, dims, preferred_element_type=jnp.float32)
        return jnp.concatenate([first[:, :half] - second[:, half:], first[:, half:] + second[:, :half]], 1)
    moments = lax.map(moment, jnp.arange(col_blocks, dtype=jnp.int32))

    def row_block(index):
        targets = lax.dynamic_slice_in_dim(tgt_geom, (index * BLK).astype(jnp.int32), BLK, 1)
        total = far_block(targets, src_geom, excite, wave_number)
        tnodes = lax.dynamic_slice_in_dim(tgt_nodes, (index * QN).astype(jnp.int32), QN, 1)
        unodes = lax.dynamic_slice_in_dim(tgt_weights, (index * BLK).astype(jnp.int32), BLK, 2)
        home = index // RBD
        for offset in range(NBAND):
            other = home + offset - NEARW
            valid = jnp.logical_and(other >= 0, other < col_blocks).astype(jnp.float32)
            clipped = jnp.clip(other, 0, col_blocks - 1).astype(jnp.int32)
            snodes = lax.dynamic_slice_in_dim(src_nodes, clipped * QN, QN, 1) * valid
            there = moments[clipped] * valid
            total = total + near_term(tnodes, snodes, there, unodes, near_order[index, offset], wave_number)
        return total
    result = lax.map(row_block, jnp.arange(row_blocks, dtype=jnp.int32))
    return result.reshape(NROWS, 2 * NEXC)
```

```python
import functools
import math

import jax
import jax.numpy as jnp
import numpy as np
from jax import lax
from jax.experimental import pallas as pl
from jax.experimental.pallas import tpu as pltpu
from jax.sharding import PartitionSpec as P

ORDERS = 3
SOFT = 0.05
FOUR_PI = 4.0 * math.pi
LANES = 128
MESH = pl.DeviceIdType.MESH
TN = (((0,), (0,)), ((), ()))


def fitted(function, terms):
    nodes = (np.cos((np.arange(terms) + 0.5) * np.pi / terms) + 1.0) / 8.0
    matrix = np.vander(nodes, terms, increasing=True)
    return [float(c) for c in np.linalg.solve(matrix, function(np.sqrt(nodes)))]


COS = fitted(lambda u: np.cos(2.0 * np.pi * u), 7)
SIN = fitted(lambda u: np.sin(2.0 * np.pi * u) / u, 7)


def horner(coefficients, y):
    total = coefficients[-1]
    for c in coefficients[-2::-1]:
        total = total * y + c
    return total


def cos_sin(turns):
    u = turns - jnp.round(turns)
    y = u * u
    return horner(COS, y), u * horner(SIN, y)


def times_i(value):
    half = value.shape[1] // 2
    swapped = jnp.concatenate([value[:, half:], value[:, :half]], 1)
    lane = lax.broadcasted_iota(jnp.int32, value.shape, 1)
    return jnp.where(lane < half, -swapped, swapped)


def split_two(value):
    high = value.astype(jnp.bfloat16)
    return high, (value - high.astype(jnp.float32)).astype(jnp.bfloat16)


def columns_of(rows):
    few, lanes = rows.shape
    pad = jnp.zeros((8 - few, lanes), jnp.float32)
    return jnp.concatenate([rows, pad], 0).T


def kernel(
    wave_ref,
    order_ref,
    tgt_ref,
    tnode_ref,
    tweight_ref,
    geom_hbm,
    excite_hbm,
    snode_hbm,
    sweight_hbm,
    out_ref,
    node_all,
    weight_all,
    geom_all,
    excite_all,
    green,
    node_send,
    weight_send,
    geom_send,
    excite_send,
    recv,
    pair_send,
    pair_recv,
):
    n_row = lax.axis_size("row")
    row = lax.axis_index("row")
    col = lax.axis_index("col")
    other = 1 - col
    band = node_all.shape[0]
    reach = (band - 1) // 2
    qn = node_all.shape[2]
    qpad = pl.cdiv(qn, LANES) * LANES
    step_nodes = qn // ORDERS
    per = excite_hbm.shape[0]
    blk = out_ref.shape[0]

    barrier = pltpu.get_barrier_semaphore()

    @pl.loop(1, n_row)
    def _(d):
        pl.semaphore_signal(
            barrier, inc=1, device_id={"row": lax.rem(row + d, n_row)}, device_id_type=MESH
        )

    pl.semaphore_signal(barrier, inc=1, device_id={"col": other}, device_id_type=MESH)

    def fill(slot):
        pltpu.make_async_copy(snode_hbm, node_all.at[slot], recv.at[0]).start()
        pltpu.make_async_copy(sweight_hbm, weight_all.at[col, slot], recv.at[1]).start()

    @pl.loop(0, band)
    def _(slot):
        block = row + slot - reach
        missing = jnp.logical_or(block < 0, block >= n_row)

        @pl.when(jnp.logical_or(missing, slot == reach))
        def _():
            fill(slot)

    pltpu.make_async_copy(geom_hbm, geom_all.at[col, row], recv.at[2]).start()
    pltpu.make_async_copy(excite_hbm, excite_all.at[col, row], recv.at[3]).start()

    pl.semaphore_wait(barrier, n_row)

    def near_copies(slot):
        to = {"row": row + reach - slot}
        nodes = pltpu.make_async_remote_copy(
            src_ref=snode_hbm,
            dst_ref=node_all.at[slot],
            send_sem=node_send.at[slot],
            recv_sem=recv.at[0],
            device_id=to,
            device_id_type=MESH,
        )
        weights = pltpu.make_async_remote_copy(
            src_ref=sweight_hbm,
            dst_ref=weight_all.at[col, slot],
            send_sem=weight_send.at[slot],
            recv_sem=recv.at[1],
            device_id=to,
            device_id_type=MESH,
        )
        return nodes, weights

    def far_copies(d):
        to = {"row": lax.rem(row + d, n_row)}
        geoms = pltpu.make_async_remote_copy(
            src_ref=geom_hbm,
            dst_ref=geom_all.at[col, row],
            send_sem=geom_send.at[d],
            recv_sem=recv.at[2],
            device_id=to,
            device_id_type=MESH,
        )
        excites = pltpu.make_async_remote_copy(
            src_ref=excite_hbm,
            dst_ref=excite_all.at[col, row],
            send_sem=excite_send.at[d],
            recv_sem=recv.at[3],
            device_id=to,
            device_id_type=MESH,
        )
        return geoms, excites

    def for_near(act):
        @pl.loop(0, band)
        def _(slot):
            goal = row + reach - slot
            inside = jnp.logical_and(goal >= 0, goal < n_row)

            @pl.when(jnp.logical_and(inside, slot != reach))
            def _():
                act(slot)

    for_near(lambda slot: near_copies(slot)[0].start())

    @pl.loop(1, n_row)
    def _(d):
        far_copies(d)[0].start()

    for_near(lambda slot: near_copies(slot)[1].start())

    @pl.loop(1, n_row)
    def _(d):
        far_copies(d)[1].start()

    def to_pair(index, buffer):
        return pltpu.make_async_remote_copy(
            src_ref=buffer.at[col],
            dst_ref=buffer.at[col],
            send_sem=pair_send.at[index],
            recv_sem=pair_recv.at[index],
            device_id={"col": other},
            device_id_type=MESH,
        )

    def from_pair(index, buffer):
        return pltpu.make_async_remote_copy(
            src_ref=buffer.at[other],
            dst_ref=buffer.at[other],
            send_sem=pair_send.at[index],
            recv_sem=pair_recv.at[index],
            device_id={"col": other},
            device_id_type=MESH,
        )

    wave = wave_ref[0]
    per_turn = wave * (0.5 / math.pi)

    tnodes = tnode_ref[...]
    tnodes = jnp.where(col == 0, tnodes[:, :qn], tnodes[:, qn:])
    if qpad > qn:
        tnodes = jnp.concatenate([tnodes, jnp.zeros((3, qpad - qn), jnp.float32)], 1)
    tcols = columns_of(tnodes)[:qn]
    t_x, t_y, t_z = (jnp.broadcast_to(tcols[:, i : i + 1], (qn, LANES)) for i in range(3))

    pltpu.make_async_copy(node_all, node_all, recv.at[0]).wait()

    @pl.loop(0, band)
    def _(slot):
        snodes = node_all[slot]
        if qpad > qn:
            snodes = jnp.concatenate([snodes, jnp.zeros((3, qpad - qn), jnp.float32)], 1)
        for part in range(qpad // LANES):
            here = slice(part * LANES, (part + 1) * LANES)
            d_x = t_x - snodes[0:1, here]
            d_y = t_y - snodes[1:2, here]
            d_z = t_z - snodes[2:3, here]
            squared = d_x * d_x + d_y * d_y + d_z * d_z + SOFT * SOFT
            inverse = lax.rsqrt(squared)
            cosine, sine = cos_sin(per_turn * (squared * inverse))
            for index, value in enumerate((inverse * cosine, inverse * sine)):
                high, low = split_two(value)
                at = index * qpad + part * LANES
                green[slot, 0, :, at : at + LANES] = high
                green[slot, 1, :, at : at + LANES] = low

    pltpu.make_async_copy(geom_all.at[col], geom_all.at[col], recv.at[2]).wait()
    to_pair(0, geom_all).start()
    pltpu.make_async_copy(weight_all.at[col], weight_all.at[col], recv.at[1]).wait()
    to_pair(1, weight_all).start()
    pltpu.make_async_copy(excite_all.at[col], excite_all.at[col], recv.at[3]).wait()
    to_pair(2, excite_all).start()
    from_pair(0, geom_all).wait_recv()

    begin = pl.multiple_of(col * blk, blk)
    gcols = columns_of(tgt_ref[:, pl.ds(begin, blk)])
    p_x, p_y, p_z, n_x, n_y, n_z = (gcols[:, i : i + 1] for i in range(6))
    pieces = LANES // per
    chunks = n_row // pieces

    def impedance(half, chunk):
        places = jnp.concatenate([geom_all[half, chunk * pieces + i] for i in range(pieces)], 1)
        d_x = p_x - places[0:1]
        d_y = p_y - places[1:2]
        d_z = p_z - places[2:3]
        squared = d_x * d_x + d_y * d_y + d_z * d_z + SOFT * SOFT
        inverse = lax.rsqrt(squared)
        radius = squared * inverse
        along = (n_x * d_x + n_y * d_y + n_z * d_z) * inverse
        scale = places[3:4] * (inverse * (1.0 / FOUR_PI))
        cosine, sine = cos_sin(per_turn * radius)
        green_re = scale * cosine
        green_im = scale * sine
        factor_re = 1.0 - along
        factor_im = -along / (wave * radius)
        kern_re = green_re * factor_re - green_im * factor_im
        kern_im = green_re * factor_im + green_im * factor_re
        return jnp.concatenate(
            [kern_re.astype(jnp.bfloat16), kern_im.astype(jnp.bfloat16)], 1
        )

    def both(rows):
        turned = times_i(rows.astype(jnp.float32)).astype(jnp.bfloat16)
        return jnp.concatenate([rows, turned], 0)

    from_pair(2, excite_all).wait_recv()

    def far_step(index, total):
        half, chunk = index // chunks, lax.rem(index, chunks)
        rows = excite_all[half, pl.ds(chunk * pieces, pieces)].reshape(LANES, blk)
        return total + jnp.dot(
            impedance(half, chunk), both(rows), preferred_element_type=jnp.float32
        )

    far = lax.fori_loop(0, 2 * chunks, far_step, jnp.zeros(out_ref.shape, jnp.float32))

    from_pair(1, weight_all).wait_recv()
    width = out_ref.shape[1]
    node_index = lax.broadcasted_iota(jnp.int32, (qpad, width), 0)

    def near_step(slot, total):
        block = row + slot - reach
        valid = jnp.logical_and(block >= 0, block < n_row)
        live = jnp.where(valid, order_ref[col, slot] * step_nodes, 0)
        source = jnp.clip(block, 0, n_row - 1)
        stack = []
        for part in range(2):
            for half in range(2):
                stack.append(weight_all[half, slot, part])
        weights = jnp.concatenate(stack, 0)
        if qpad > qn:
            weights = jnp.concatenate(
                [weights, jnp.zeros((weights.shape[0], qpad - qn), jnp.bfloat16)], 1
            )
        rows = jnp.concatenate([excite_all[half, source] for half in range(2)], 0)
        moments = lax.dot_general(weights, both(rows), TN, preferred_element_type=jnp.float32)
        moments = jnp.where(node_index < live, moments * (1.0 / FOUR_PI), 0.0)
        full = jnp.concatenate([moments, times_i(moments)], 0)
        high, low = split_two(full)
        product = jnp.dot(
            green[slot, 0],
            jnp.concatenate([high, low], 1),
            preferred_element_type=jnp.float32,
        )
        product = (
            product[:, :width]
            + product[:, width:]
            + jnp.dot(green[slot, 1], high, preferred_element_type=jnp.float32)
        )
        return total + jnp.where(node_index[:qn] < live, product, 0.0)

    inner = lax.fori_loop(0, band, near_step, jnp.zeros((qn, width), jnp.float32))
    tests = jnp.concatenate(
        [tweight_ref[0, :, pl.ds(begin, blk)], tweight_ref[1, :, pl.ds(begin, blk)]], 0
    )
    high, low = split_two(jnp.concatenate([inner, times_i(inner)], 0))
    product = lax.dot_general(
        tests, jnp.concatenate([high, low], 1), TN, preferred_element_type=jnp.float32
    )
    out_ref[...] = far + (product[:, :width] + product[:, width:])

    for_near(lambda slot: [copy.wait_send() for copy in near_copies(slot)])

    @pl.loop(1, n_row)
    def _(d):
        for copy in far_copies(d):
            copy.wait_send()

    for index, buffer in enumerate((geom_all, weight_all, excite_all)):
        to_pair(index, buffer).wait_send()


def on_device(
    wavenumber,
    tgt_geom,
    src_geom,
    excite,
    tgt_nodes,
    src_nodes,
    tgt_weights,
    src_weights,
    near_order,
):
    n_row = lax.axis_size("row")
    band = near_order.shape[1]
    blk = tgt_geom.shape[1] // lax.axis_size("col")
    qn = src_nodes.shape[1]
    qpad = -(-qn // LANES) * LANES
    excite_rows = excite.T
    weight_rows = src_weights.transpose(0, 2, 1)
    vmem = pl.BlockSpec(memory_space=pltpu.VMEM)
    smem = pl.BlockSpec(memory_space=pltpu.SMEM)
    hbm = pl.BlockSpec(memory_space=pl.ANY)
    dma = pltpu.SemaphoreType.DMA
    return pl.pallas_call(
        kernel,
        out_shape=jax.ShapeDtypeStruct((blk, excite.shape[0]), jnp.float32),
        in_specs=[smem, smem, vmem, vmem, vmem, hbm, hbm, hbm, hbm],
        out_specs=vmem,
        scratch_shapes=[
            pltpu.VMEM((band,) + src_nodes.shape, jnp.float32),
            pltpu.VMEM((2, band) + weight_rows.shape, jnp.bfloat16),
            pltpu.VMEM((2, n_row) + src_geom.shape, jnp.float32),
            pltpu.VMEM((2, n_row) + excite_rows.shape, jnp.bfloat16),
            pltpu.VMEM((band, 2, qn, 2 * qpad), jnp.bfloat16),
            dma((band,)),
            dma((band,)),
            dma((n_row,)),
            dma((n_row,)),
            dma((4,)),
            dma((3,)),
            dma((3,)),
        ],
        compiler_params=pltpu.CompilerParams(collective_id=0, has_side_effects=True),
        name="slab",
    )(
        wavenumber,
        near_order,
        tgt_geom,
        tgt_nodes,
        tgt_weights,
        src_geom,
        excite_rows,
        src_nodes,
        weight_rows,
    )


def solution(mesh):
    return jax.shard_map(
        on_device,
        mesh=mesh,
        in_specs=(
            P("groups"),
            P(None, ("groups", "row")),
            P(None, ("groups", "row", "col")),
            P(None, ("groups", "row", "col")),
            P(None, ("groups", "row")),
            P(None, ("groups", "row")),
            P(None, None, ("groups", "row")),
            P(None, None, ("groups", "row", "col")),
            P(("groups", "row"), None),
        ),
        out_specs=P(("groups", "row", "col"), None),
        check_vma=False,
    )
```

```python
import functools
import math

import jax
import jax.numpy as jnp
import numpy as np
from jax import lax
from jax.experimental import pallas as pl
from jax.experimental.pallas import tpu as pltpu
from jax.sharding import PartitionSpec as P

ORDERS = 3
SOFT = 0.05
FOUR_PI = 4.0 * math.pi
LANES = 128
MESH = pl.DeviceIdType.MESH
TN = (((0,), (0,)), ((), ()))
NT = (((1,), (1,)), ((), ()))


def fitted(function, terms):
    nodes = (np.cos((np.arange(terms) + 0.5) * np.pi / terms) + 1.0) / 8.0
    matrix = np.vander(nodes, terms, increasing=True)
    return [float(c) for c in np.linalg.solve(matrix, function(np.sqrt(nodes)))]


COS = fitted(lambda u: np.cos(2.0 * np.pi * u), 7)
SIN = fitted(lambda u: np.sin(2.0 * np.pi * u) / u, 7)


def horner(coefficients, y):
    total = coefficients[-1]
    for c in coefficients[-2::-1]:
        total = total * y + c
    return total


def cos_sin(turns):
    u = turns - jnp.round(turns)
    y = u * u
    return horner(COS, y), u * horner(SIN, y)


def times_i(value):
    half = value.shape[1] // 2
    swapped = jnp.concatenate([value[:, half:], value[:, :half]], 1)
    lane = lax.broadcasted_iota(jnp.int32, value.shape, 1)
    return jnp.where(lane < half, -swapped, swapped)


def split_two(value):
    high = value.astype(jnp.bfloat16)
    return high, (value - high.astype(jnp.float32)).astype(jnp.bfloat16)


def columns_of(rows):
    few, lanes = rows.shape
    pad = jnp.zeros((8 - few, lanes), jnp.float32)
    return jnp.concatenate([rows, pad], 0).T


def kernel(
    wave_hbm,
    order_hbm,
    tgt_hbm,
    tnode_hbm,
    tweight_hbm,
    geom_hbm,
    excite_hbm,
    snode_hbm,
    sweight_hbm,
    out_ref,
    node_all,
    weight_all,
    geom_all,
    excite_all,
    green_high,
    green_low,
    wave_ref,
    order_ref,
    tgt_ref,
    tnode_ref,
    tweight_ref,
    node_own,
    local,
    node_send,
    weight_send,
    geom_send,
    excite_send,
    recv,
    weight_recv,
    weight_pair,
    weight_back,
    pair_send,
    pair_recv,
):
    n_row = lax.axis_size("row")
    row = lax.axis_index("row")
    col = lax.axis_index("col")
    other = 1 - col
    band = node_all.shape[0]
    reach = (band - 1) // 2
    qn = node_all.shape[2]
    qpad = pl.cdiv(qn, LANES) * LANES
    step_nodes = qn // ORDERS
    per = excite_hbm.shape[0]
    blk = out_ref.shape[0]

    barrier = pltpu.get_barrier_semaphore()

    @pl.loop(1, n_row)
    def _(d):
        pl.semaphore_signal(
            barrier, inc=1, device_id={"row": lax.rem(row + d, n_row)}, device_id_type=MESH
        )

    pl.semaphore_signal(barrier, inc=1, device_id={"col": other}, device_id_type=MESH)

    loads = [
        pltpu.make_async_copy(here, there, local.at[index])
        for index, (here, there) in enumerate(
            (
                (wave_hbm, wave_ref),
                (tnode_hbm, tnode_ref),
                (order_hbm, order_ref),
                (tgt_hbm, tgt_ref),
                (tweight_hbm, tweight_ref),
            )
        )
    ]
    own_nodes = pltpu.make_async_copy(snode_hbm, node_own, local.at[len(loads)])
    own_nodes.start()
    for load in loads:
        load.start()

    def fill(slot):
        pltpu.make_async_copy(snode_hbm, node_all.at[slot], recv.at[0]).start()
        pltpu.make_async_copy(sweight_hbm, weight_all.at[col, slot], weight_recv.at[slot]).start()

    @pl.loop(0, band)
    def _(slot):
        block = row + slot - reach
        missing = jnp.logical_or(block < 0, block >= n_row)

        @pl.when(jnp.logical_or(missing, slot == reach))
        def _():
            fill(slot)

    pltpu.make_async_copy(geom_hbm, geom_all.at[col, row], recv.at[2]).start()
    pltpu.make_async_copy(excite_hbm, excite_all.at[col, row], recv.at[3]).start()

    def near_copies(slot):
        to = {"row": row + reach - slot}
        nodes = pltpu.make_async_remote_copy(
            src_ref=snode_hbm,
            dst_ref=node_all.at[slot],
            send_sem=node_send.at[slot],
            recv_sem=recv.at[0],
            device_id=to,
            device_id_type=MESH,
        )
        weights = pltpu.make_async_remote_copy(
            src_ref=sweight_hbm,
            dst_ref=weight_all.at[col, slot],
            send_sem=weight_send.at[slot],
            recv_sem=weight_recv.at[slot],
            device_id=to,
            device_id_type=MESH,
        )
        return nodes, weights

    def far_copies(d):
        to = {"row": lax.rem(row + d, n_row)}
        geoms = pltpu.make_async_remote_copy(
            src_ref=geom_hbm,
            dst_ref=geom_all.at[col, row],
            send_sem=geom_send.at[d],
            recv_sem=recv.at[2],
            device_id=to,
            device_id_type=MESH,
        )
        excites = pltpu.make_async_remote_copy(
            src_ref=excite_hbm,
            dst_ref=excite_all.at[col, row],
            send_sem=excite_send.at[d],
            recv_sem=recv.at[3],
            device_id=to,
            device_id_type=MESH,
        )
        return geoms, excites

    def for_near(act):
        @pl.loop(0, band)
        def _(slot):
            goal = row + reach - slot
            inside = jnp.logical_and(goal >= 0, goal < n_row)

            @pl.when(jnp.logical_and(inside, slot != reach))
            def _():
                act(slot)

    def weight_to_pair(slot, half):
        return pltpu.make_async_remote_copy(
            src_ref=weight_all.at[half, slot],
            dst_ref=weight_all.at[half, slot],
            send_sem=weight_pair.at[slot],
            recv_sem=weight_back.at[slot],
            device_id={"col": other},
            device_id_type=MESH,
        )

    def to_pair(index, buffer):
        return pltpu.make_async_remote_copy(
            src_ref=buffer.at[col],
            dst_ref=buffer.at[col],
            send_sem=pair_send.at[index],
            recv_sem=pair_recv.at[index],
            device_id={"col": other},
            device_id_type=MESH,
        )

    def from_pair(index, buffer):
        return pltpu.make_async_remote_copy(
            src_ref=buffer.at[other],
            dst_ref=buffer.at[other],
            send_sem=pair_send.at[index],
            recv_sem=pair_recv.at[index],
            device_id={"col": other},
            device_id_type=MESH,
        )

    for load in loads[:3]:
        load.wait()
    wave = wave_ref[0]
    per_turn = wave * (0.5 / math.pi)

    tnodes = tnode_ref[...]
    tnodes = jnp.where(col == 0, tnodes[:, :qn], tnodes[:, qn:])
    if qpad > qn:
        tnodes = jnp.concatenate([tnodes, jnp.zeros((3, qpad - qn), jnp.float32)], 1)
    tcols = columns_of(tnodes)[:qn]
    t_x, t_y, t_z = (jnp.broadcast_to(tcols[:, i : i + 1], (qn, LANES)) for i in range(3))

    point = lax.broadcasted_iota(jnp.int32, (qn, LANES), 0)

    def order_of(slot):
        block = row + slot - reach
        valid = jnp.logical_and(block >= 0, block < n_row)
        return jnp.where(valid, order_ref[col, slot] * step_nodes, 0)

    def green_of(slot, snodes):
        live = point < order_of(slot)
        if qpad > qn:
            snodes = jnp.concatenate([snodes, jnp.zeros((3, qpad - qn), jnp.float32)], 1)
        for part in range(qpad // LANES):
            here = slice(part * LANES, (part + 1) * LANES)
            d_x = t_x - snodes[0:1, here]
            d_y = t_y - snodes[1:2, here]
            d_z = t_z - snodes[2:3, here]
            squared = d_x * d_x + d_y * d_y + d_z * d_z + SOFT * SOFT
            inverse = lax.rsqrt(squared)
            cosine, sine = cos_sin(per_turn * (squared * inverse))
            inverse = jnp.where(live, inverse, 0.0)
            for index, value in enumerate((inverse * cosine, inverse * sine)):
                high, low = split_two(value)
                at = pl.multiple_of((2 * slot + index) * qpad + part * LANES, LANES)
                green_high[:, pl.ds(at, LANES)] = high
                green_low[:, pl.ds(at, LANES)] = low

    own_nodes.wait()
    green_of(reach, node_own[...])

    pl.semaphore_wait(barrier, n_row)

    for_near(lambda slot: near_copies(slot)[0].start())

    @pl.loop(1, n_row)
    def _(d):
        far_copies(d)[0].start()

    for_near(lambda slot: near_copies(slot)[1].start())

    @pl.loop(1, n_row)
    def _(d):
        far_copies(d)[1].start()

    pltpu.make_async_copy(node_all, node_all, recv.at[0]).wait()

    def green_some(begin, end):
        @pl.loop(begin, end)
        def _(slot):
            block = row + slot - reach
            needed = jnp.logical_and(block >= 0, block < n_row)

            @pl.when(jnp.logical_and(needed, slot != reach))
            def _():
                green_of(slot, node_all[slot])

            @pl.when(jnp.logical_not(needed))
            def _():
                at = pl.ds(pl.multiple_of(2 * slot * qpad, LANES), 2 * qpad)
                green_high[:, at] = jnp.zeros((qn, 2 * qpad), jnp.bfloat16)
                green_low[:, at] = jnp.zeros((qn, 2 * qpad), jnp.bfloat16)

    green_some(0, (band - 2))
    pltpu.make_async_copy(geom_all.at[col], geom_all.at[col], recv.at[2]).wait()
    to_pair(0, geom_all).start()

    @pl.loop(0, band)
    def _(slot):
        pltpu.make_async_copy(
            weight_all.at[col, slot], weight_all.at[col, slot], weight_recv.at[slot]
        ).wait()
        weight_to_pair(slot, col).start()

    pltpu.make_async_copy(excite_all.at[col], excite_all.at[col], recv.at[3]).wait()
    to_pair(1, excite_all).start()
    green_some((band - 2), band)
    from_pair(0, geom_all).wait_recv()

    loads[3].wait()
    begin = pl.multiple_of(col * blk, blk)
    gcols = columns_of(tgt_ref[:, pl.ds(begin, blk)])
    p_x, p_y, p_z, n_x, n_y, n_z = (gcols[:, i : i + 1] for i in range(6))
    pieces = LANES // per
    chunks = n_row // pieces

    def impedance(half, chunk):
        places = jnp.concatenate([geom_all[half, chunk * pieces + i] for i in range(pieces)], 1)
        d_x = p_x - places[0:1]
        d_y = p_y - places[1:2]
        d_z = p_z - places[2:3]
        squared = d_x * d_x + d_y * d_y + d_z * d_z + SOFT * SOFT
        inverse = lax.rsqrt(squared)
        radius = squared * inverse
        along = (n_x * d_x + n_y * d_y + n_z * d_z) * inverse
        scale = places[3:4] * (inverse * (1.0 / FOUR_PI))
        cosine, sine = cos_sin(per_turn * radius)
        green_re = scale * cosine
        green_im = scale * sine
        factor_re = 1.0 - along
        factor_im = -along / (wave * radius)
        kern_re = green_re * factor_re - green_im * factor_im
        kern_im = green_re * factor_im + green_im * factor_re
        return jnp.concatenate(
            [kern_re.astype(jnp.bfloat16), kern_im.astype(jnp.bfloat16)], 1
        )

    def both(rows):
        turned = times_i(rows.astype(jnp.float32)).astype(jnp.bfloat16)
        return jnp.concatenate([rows, turned], 0)

    from_pair(1, excite_all).wait_recv()

    def far_step(index, total):
        half, chunk = index // chunks, lax.rem(index, chunks)
        rows = excite_all[half, pl.ds(chunk * pieces, pieces)].reshape(LANES, blk)
        return total + jnp.dot(
            impedance(half, chunk), both(rows), preferred_element_type=jnp.float32
        )

    far = lax.fori_loop(0, 2 * chunks, far_step, jnp.zeros(out_ref.shape, jnp.float32))

    width = out_ref.shape[1]

    lane = lax.broadcasted_iota(jnp.int32, (2 * per, qpad), 1)
    applied, sources = [], []
    for slot in range(band):
        weight_to_pair(slot, other).wait_recv()
        live = lane < order_of(slot)
        basis = []
        for part in range(2):
            value = jnp.concatenate([weight_all[half, slot, part] for half in range(2)], 0)
            if qpad > qn:
                value = jnp.concatenate(
                    [value, jnp.zeros((2 * per, qpad - qn), jnp.bfloat16)], 1
                )
            basis.append(jnp.where(live, value.astype(jnp.float32), 0.0))
        stacked = jnp.concatenate(
            [
                jnp.concatenate([basis[0], -basis[1]], 1),
                jnp.concatenate([basis[1], basis[0]], 1),
            ],
            0,
        ).astype(jnp.bfloat16)
        here = slice(2 * slot * qpad, 2 * (slot + 1) * qpad)
        applied.append(
            lax.dot_general(green_high[:, here], stacked, NT, preferred_element_type=jnp.float32)
            + lax.dot_general(green_low[:, here], stacked, NT, preferred_element_type=jnp.float32)
        )
        source = jnp.clip(row + slot - reach, 0, n_row - 1)
        sources.append(both(jnp.concatenate([excite_all[half, source] for half in range(2)], 0)))
    high, low = split_two(jnp.concatenate(applied, 1))
    sources = jnp.concatenate(sources, 0)
    inner = jnp.dot(high, sources, preferred_element_type=jnp.float32) + jnp.dot(
        low, sources, preferred_element_type=jnp.float32
    )
    inner = inner * (1.0 / FOUR_PI)
    loads[4].wait()
    tests = jnp.concatenate(
        [tweight_ref[0, :, pl.ds(begin, blk)], tweight_ref[1, :, pl.ds(begin, blk)]], 0
    )
    high, low = split_two(jnp.concatenate([inner, times_i(inner)], 0))
    product = lax.dot_general(
        tests, jnp.concatenate([high, low], 1), TN, preferred_element_type=jnp.float32
    )
    out_ref[...] = far + (product[:, :width] + product[:, width:])

    for_near(lambda slot: [copy.wait_send() for copy in near_copies(slot)])

    @pl.loop(1, n_row)
    def _(d):
        for copy in far_copies(d):
            copy.wait_send()

    @pl.loop(0, band)
    def _(slot):
        weight_to_pair(slot, col).wait_send()

    for index, buffer in enumerate((geom_all, excite_all)):
        to_pair(index, buffer).wait_send()


def on_device(
    wavenumber,
    tgt_geom,
    src_geom,
    excite,
    tgt_nodes,
    src_nodes,
    tgt_weights,
    src_weights,
    near_order,
):
    n_row = lax.axis_size("row")
    band = near_order.shape[1]
    blk = tgt_geom.shape[1] // lax.axis_size("col")
    qn = src_nodes.shape[1]
    qpad = -(-qn // LANES) * LANES
    excite_rows = excite.T
    weight_rows = src_weights.transpose(0, 2, 1)
    vmem = pl.BlockSpec(memory_space=pltpu.VMEM)
    hbm = pl.BlockSpec(memory_space=pl.ANY)
    dma = pltpu.SemaphoreType.DMA
    return pl.pallas_call(
        kernel,
        out_shape=jax.ShapeDtypeStruct((blk, excite.shape[0]), jnp.float32),
        in_specs=[hbm] * 9,
        out_specs=vmem,
        scratch_shapes=[
            pltpu.VMEM((band,) + src_nodes.shape, jnp.float32),
            pltpu.VMEM((2, band) + weight_rows.shape, jnp.bfloat16),
            pltpu.VMEM((2, n_row) + src_geom.shape, jnp.float32),
            pltpu.VMEM((2, n_row) + excite_rows.shape, jnp.bfloat16),
            pltpu.VMEM((qn, band * 2 * qpad), jnp.bfloat16),
            pltpu.VMEM((qn, band * 2 * qpad), jnp.bfloat16),
            pltpu.SMEM(wavenumber.shape, jnp.float32),
            pltpu.SMEM(near_order.shape, jnp.int32),
            pltpu.VMEM(tgt_geom.shape, jnp.float32),
            pltpu.VMEM(tgt_nodes.shape, jnp.float32),
            pltpu.VMEM(tgt_weights.shape, jnp.bfloat16),
            pltpu.VMEM(src_nodes.shape, jnp.float32),
            dma((6,)),
            dma((band,)),
            dma((band,)),
            dma((n_row,)),
            dma((n_row,)),
            dma((4,)),
            dma((band,)),
            dma((band,)),
            dma((band,)),
            dma((2,)),
            dma((2,)),
        ],
        compiler_params=pltpu.CompilerParams(collective_id=0, has_side_effects=True),
        name="slab",
    )(
        wavenumber,
        near_order,
        tgt_geom,
        tgt_nodes,
        tgt_weights,
        src_geom,
        excite_rows,
        src_nodes,
        weight_rows,
    )


def solution(mesh):
    return jax.shard_map(
        on_device,
        mesh=mesh,
        in_specs=(
            P("groups"),
            P(None, ("groups", "row")),
            P(None, ("groups", "row", "col")),
            P(None, ("groups", "row", "col")),
            P(None, ("groups", "row")),
            P(None, ("groups", "row")),
            P(None, None, ("groups", "row")),
            P(None, None, ("groups", "row", "col")),
            P(("groups", "row"), None),
        ),
        out_specs=P(("groups", "row", "col"), None),
        check_vma=False,
    )
```
